32 devices in a mesh: rep: 8 (over y, x, core), shard: 4 (over z).
Axes of the slice: x: 2, y: 2, z: 4, core: 2. Of those that a mesh axis runs over, the one named last changes fastest.
Arguments:
- tokens_in: float32 [32, 256, 768], P(('rep', 'shard')), may hold values from -6 to 6
- cotangent: float32 [32, 256, 768], P(('rep', 'shard')), may hold values from -6 to 6
- attention_master: float32 [3072, 768], P(('rep', 'shard')), may hold values from -1.1547005 to 1.1547005
- feedforward_master: float32 [6144, 768], P(('rep', 'shard')), may hold values from -0.21875 to 0.21875
- vector_master: float32 [9216], P(('rep', 'shard')), may hold values from -0.5 to 1.3
- attention_first: float32 [3072, 768], P(('rep', 'shard')), may hold values from -64 to 64
- attention_second: float32 [3072, 768], P(('rep', 'shard')), may hold values from 40.96 to 1638.4
- feedforward_first: float32 [6144, 768], P(('rep', 'shard')), may hold values from -16 to 16
- feedforward_second: float32 [6144, 768], P(('rep', 'shard')), may hold values from 4.096 to 81.92
- vector_first: float32 [9216], P(('rep', 'shard')), may hold values from -16 to 16
- vector_second: float32 [9216], P(('rep', 'shard')), may hold values from 4.096 to 81.92
Outputs:
- block_out: float32 [32, 256, 768], P(('rep', 'shard'))
- input_grad: float32 [32, 256, 768], P(('rep', 'shard'))
- attention_grad: float32 [3072, 768], P(('rep', 'shard'))
- feedforward_grad: float32 [6144, 768], P(('rep', 'shard'))
- vector_grad: float32 [9216], P(('rep', 'shard'))
- attention_new: float32 [3072, 768], P(('rep', 'shard'))
- feedforward_new: float32 [6144, 768], P(('rep', 'shard'))
- vector_new: float32 [9216], P(('rep', 'shard'))
- attention_first_new: float32 [3072, 768], P(('rep', 'shard'))
- attention_second_new: float32 [3072, 768], P(('rep', 'shard'))
- feedforward_first_new: float32 [6144, 768], P(('rep', 'shard'))
- feedforward_second_new: float32 [6144, 768], P(('rep', 'shard'))
- vector_first_new: float32 [9216], P(('rep', 'shard'))
- vector_second_new: float32 [9216], P(('rep', 'shard'))
The draws below stay inside these ranges and needn't reach their ends.
All inputs are finite; a program needn't handle non-finite values.
Results may differ from the reference program's by a relative error of at most 0.0095.
The reference program's roundings to bfloat16 on the way count: a program that leaves them out, or rounds other values in their place, can miss the bound.
Values may be sent and summed in bfloat16 or wider, within the bound.
No kernel may reach another device: no remote copies, remote signals or barrier semaphores. Data moves between devices by JAX's collectives and lax.ppermute only.
A program may use at most 128 MiB of HBM per device.

```python
import math
import jax
import jax.numpy as jnp
from jax import lax

D = 768
HEADS = 12
HD = 64
FF = 3072
FRAMES = 256
ADAM_STEP = 2
CLIPS = 32
VEC = 9216


def draw_attention_master(key, part):
    base = jax.random.truncated_normal(key, -4.0, 4.0, (4 * D, D), jnp.float32) * D ** (-0.5)
    factor = jnp.where(jnp.arange(4 * D) >= 3 * D, 8.0, 1.0)[:, None]
    base = base * factor
    return base


def draw_vector_master(key, part):
    length = 8 * D + FF
    column = jnp.arange(length) % 12
    spread = jax.random.uniform(key, (length,), jnp.float32, -1.0, 1.0)
    is_gain = (column == 0) | (column == 5)
    return jnp.where(is_gain, 1.0 + 0.3 * spread, 0.5 * spread)


def strengthened(values, stream_key, source, target, blocks, factor):
    owner, partner = [(jnp.arange(values.shape[axis_at]) // (values.shape[axis_at] // blocks)).reshape([-1 if axis == axis_at else 1 for axis in range(values.ndim)]) for axis_at in (source, target)]
    chosen = jax.random.permutation(stream_key, blocks)[partner]
    strong = (owner == chosen) | (owner == (partner + blocks // 2) % blocks)
    return jnp.where(strong, factor * values, values)


def block_levels(stream_key, extent, shards, least, high):
    loudness = 1.0
    for position, blocks in shards:
        steps = jax.random.uniform(jax.random.fold_in(jax.random.fold_in(stream_key, 6), position), (blocks,), jnp.float32, least / len(shards), high / len(shards))
        loudness = loudness * jnp.repeat(jnp.exp(steps), extent[position] // blocks).reshape((-1,) + (1,) * (len(extent) - 1 - position))
    return loudness


def centred(own_key, dims, scale, most, shards=(), kind=jnp.bfloat16):
    loudness = block_levels(own_key, dims, shards, -0.22, 0.18) if shards else 1.0
    result = jax.random.normal(own_key, dims, jnp.float32) * scale * loudness
    return jnp.minimum(jnp.maximum(result, -most), most).astype(kind)


def heavy_noise(stream_key, extent, deviation, most, shards, heavy, kind=jnp.bfloat16):
    entries = deviation * jax.random.normal(stream_key, extent, jnp.float32)
    if shards:
        entries = entries * block_levels(stream_key, extent, shards, -0.22, 0.18)
    return jnp.clip(strengthened(entries, jax.random.fold_in(stream_key, 3), *heavy), -most, most).astype(kind)


def setup_inputs(seed: int = 0) -> dict:
    streams_of = jax.random.split(jax.random.key(seed), 12)
    tokens_in = centred(streams_of[0], (CLIPS, FRAMES, D), 1.0, 6.0, ((0, 32),), jnp.float32)
    cotangent = heavy_noise(streams_of[1], (CLIPS, FRAMES, D), 1.0, 6.0, ((0, 32),), (0, 2, 32, 2.75), jnp.float32)
    attention_master = draw_attention_master(jax.random.fold_in(streams_of[11], 71), 0)
    feedforward_master = centred(streams_of[3], (2 * FF, D), D ** -0.5, 0.21875, ((0, 32),), jnp.float32)
    vector_master = draw_vector_master(jax.random.fold_in(streams_of[11], 71), 0)
    attention_first = centred(streams_of[5], (4 * D, D), (0.12 * (CLIPS * FRAMES) ** 0.5), 64.0, ((0, 32),), jnp.float32)
    attention_second = jnp.clip(jnp.exp(math.log(1638.4) - 3.6888795 * jax.random.uniform(streams_of[6], (4 * D, D), jnp.float32) ** block_levels(streams_of[6], (4 * D, D), ((0, 32),), -0.2, 0.2)), 40.96, 1638.4)
    feedforward_first = centred(streams_of[7], (2 * FF, D), (0.03 * (CLIPS * FRAMES) ** 0.5), 16.0, ((0, 32),), jnp.float32)
    feedforward_second = jnp.clip(jnp.exp(math.log(81.92) - 2.9957322 * jax.random.uniform(streams_of[8], (2 * FF, D), jnp.float32) ** block_levels(streams_of[8], (2 * FF, D), ((0, 32),), -0.2, 0.2)), 4.096, 81.92)
    vector_first = centred(streams_of[9], (VEC,), (0.03 * (CLIPS * FRAMES) ** 0.5), 16.0, ((0, 32),), jnp.float32)
    vector_second = jnp.clip(jnp.exp(math.log(81.92) - 2.9957322 * jax.random.uniform(streams_of[10], (VEC,), jnp.float32) ** block_levels(streams_of[10], (VEC,), ((0, 32),), -0.2, 0.2)), 4.096, 81.92)
    return dict(tokens_in=tokens_in, cotangent=cotangent, attention_master=attention_master, feedforward_master=feedforward_master, vector_master=vector_master, attention_first=attention_first, attention_second=attention_second, feedforward_first=feedforward_first, feedforward_second=feedforward_second, vector_first=vector_first, vector_second=vector_second)


EPS_NORM = 1e-05
EPS_ADAM = 1e-08
BETA_ONE = 0.9
BETA_TWO = 0.95
RATE_MATRIX = 0.01
RATE_VECTOR = 0.05
DECAY_MATRIX = 0.01
HIGH = lax.Precision.HIGHEST

def mix(form, left, right):
    return jnp.einsum(form, left.astype(jnp.float32), right.astype(jnp.float32), precision=HIGH)

def times_trans(left, right):
    return lax.dot_general(left, right, (((1,), (1,)), ((), ())), preferred_element_type=jnp.float32)

def outer_sum(left, right):
    return lax.dot_general(left, right, (((0,), (0,)), ((), ())), preferred_element_type=jnp.float32)

def layer_norm(field, gain, shift):
    center = field - lax.optimization_barrier(jnp.mean(field, axis=-1, keepdims=True))
    inverse = lax.rsqrt(lax.optimization_barrier(jnp.mean(center * center, axis=-1, keepdims=True)) + EPS_NORM)
    normed = center * inverse
    return (normed * gain + shift, normed, inverse)

def norm_back(upstream, normed, inverse, gain):
    scaled = upstream * gain
    return inverse * (scaled - lax.optimization_barrier(jnp.mean(scaled, axis=-1, keepdims=True)) - normed * lax.optimization_barrier(jnp.mean(scaled * normed, axis=-1, keepdims=True)))

def gelu_value(pre):
    return 0.5 * pre * (1.0 + lax.erf(pre * 0.7071067811865476))

def gelu_slope(pre):
    return 0.5 * (1.0 + lax.erf(pre * 0.7071067811865476)) + pre * jnp.exp(-0.5 * pre * pre) * 0.3989422804014327

def clip_pass(tokens, upstream, attention, feedforward, vector):
    frames = tokens.shape[0]
    scale = HD ** (-0.5)
    vec = vector.astype(jnp.float32).reshape(D, 12)
    gain_one = vec[:, 0]
    shift_one = vec[:, 1]
    bias_query = vec[:, 2]
    bias_value = vec[:, 3]
    bias_out = vec[:, 4]
    gain_two = vec[:, 5]
    shift_two = vec[:, 6]
    bias_down = vec[:, 7]
    bias_up = vec[:, 8:].reshape(FF)
    w_query = attention[0:D]
    w_key = attention[D:2 * D]
    w_value = attention[2 * D:3 * D]
    w_out = attention[3 * D:]
    w_up = feedforward[0:FF]
    w_down = feedforward[FF:]
    normed_out, normed_one, inverse_one = layer_norm(tokens, gain_one, shift_one)
    inputs_bf = normed_out.astype(jnp.bfloat16)
    queries = (times_trans(inputs_bf, w_query) + bias_query).astype(jnp.bfloat16).reshape(frames, HEADS, HD)
    keys_bf = times_trans(inputs_bf, w_key).astype(jnp.bfloat16).reshape(frames, HEADS, HD)
    values_bf = (times_trans(inputs_bf, w_value) + bias_value).astype(jnp.bfloat16).reshape(frames, HEADS, HD)
    scores = mix('qhd,khd->hqk', queries, keys_bf) * scale
    top = lax.optimization_barrier(jnp.max(scores, axis=-1, keepdims=True))
    lse = top + jnp.log(lax.optimization_barrier(jnp.sum(jnp.exp(scores - top), axis=-1, keepdims=True)))
    weights_bf = jnp.exp(scores - lse).astype(jnp.bfloat16)
    context = mix('hqk,khd->qhd', weights_bf, values_bf).reshape(frames, D).astype(jnp.bfloat16)
    resid = tokens + times_trans(context, w_out) + bias_out
    normed_out_two, normed_two, inverse_two = layer_norm(resid, gain_two, shift_two)
    mlp_in = normed_out_two.astype(jnp.bfloat16)
    pre = times_trans(mlp_in, w_up) + bias_up
    active = gelu_value(pre).astype(jnp.bfloat16)
    output = resid + jnp.dot(active, w_down, preferred_element_type=jnp.float32) + bias_down
    upstream_bf = upstream.astype(jnp.bfloat16)
    grad_down = outer_sum(active, upstream_bf)
    grad_bias_down = lax.optimization_barrier(jnp.sum(upstream, axis=0))
    grad_pre = times_trans(upstream_bf, w_down) * gelu_slope(pre)
    grad_pre_bf = grad_pre.astype(jnp.bfloat16)
    grad_up = outer_sum(grad_pre_bf, mlp_in)
    grad_bias_up = lax.optimization_barrier(jnp.sum(grad_pre, axis=0))
    grad_normed_two = jnp.dot(grad_pre_bf, w_up, preferred_element_type=jnp.float32)
    grad_gain_two = lax.optimization_barrier(jnp.sum(grad_normed_two * normed_two, axis=0))
    grad_shift_two = lax.optimization_barrier(jnp.sum(grad_normed_two, axis=0))
    grad_resid = upstream + norm_back(grad_normed_two, normed_two, inverse_two, gain_two)
    resid_bf = grad_resid.astype(jnp.bfloat16)
    grad_out = outer_sum(resid_bf, context)
    grad_bias_out = lax.optimization_barrier(jnp.sum(grad_resid, axis=0))
    grad_context = jnp.dot(resid_bf, w_out, preferred_element_type=jnp.float32).astype(jnp.bfloat16)
    again = mix('qhd,khd->hqk', queries, keys_bf) * scale
    probs = jnp.exp(again - lse)
    probs_bf = probs.astype(jnp.bfloat16)
    context_heads = grad_context.reshape(frames, HEADS, HD)
    delta = lax.optimization_barrier(jnp.sum(grad_context.astype(jnp.float32).reshape(frames, HEADS, HD) * context.astype(jnp.float32).reshape(frames, HEADS, HD), axis=-1))
    delta = jnp.transpose(delta)[:, :, None]
    grad_values = mix('hqk,qhd->khd', probs_bf, context_heads).reshape(frames, D)
    grad_probs = mix('qhd,khd->hqk', context_heads, values_bf)
    grad_scores = (probs * (grad_probs - delta)).astype(jnp.bfloat16)
    grad_queries = (mix('hqk,khd->qhd', grad_scores, keys_bf) * scale).reshape(frames, D)
    grad_keys = (mix('hqk,qhd->khd', grad_scores, queries) * scale).reshape(frames, D)
    grad_bias_query = lax.optimization_barrier(jnp.sum(grad_queries, axis=0))
    grad_bias_value = lax.optimization_barrier(jnp.sum(grad_values, axis=0))
    queries_grad_bf = grad_queries.astype(jnp.bfloat16)
    keys_grad_bf = grad_keys.astype(jnp.bfloat16)
    values_grad_bf = grad_values.astype(jnp.bfloat16)
    grad_wq = outer_sum(queries_grad_bf, inputs_bf)
    grad_wk = outer_sum(keys_grad_bf, inputs_bf)
    grad_wv = outer_sum(values_grad_bf, inputs_bf)
    grad_normed_one = jnp.dot(queries_grad_bf, w_query, preferred_element_type=jnp.float32) + jnp.dot(keys_grad_bf, w_key, preferred_element_type=jnp.float32) + jnp.dot(values_grad_bf, w_value, preferred_element_type=jnp.float32)
    grad_gain_one = lax.optimization_barrier(jnp.sum(grad_normed_one * normed_one, axis=0))
    grad_shift_one = lax.optimization_barrier(jnp.sum(grad_normed_one, axis=0))
    grad_tokens = grad_resid + norm_back(grad_normed_one, normed_one, inverse_one, gain_one)
    attention_part = jnp.concatenate([grad_wq, grad_wk, grad_wv, grad_out], axis=0)
    feedforward_part = jnp.concatenate([grad_up, grad_down], axis=0)
    per_feature = jnp.stack([grad_gain_one, grad_shift_one, grad_bias_query, grad_bias_value, grad_bias_out, grad_gain_two, grad_shift_two, grad_bias_down], axis=1)
    vector_part = jnp.concatenate([per_feature, grad_bias_up.reshape(D, FF // D)], axis=1).reshape(-1)
    return (output, grad_tokens, (attention_part, feedforward_part, vector_part))

def adam_update(master, first, second, grad, rate, decay):
    first_new = BETA_ONE * first + (1.0 - BETA_ONE) * grad
    second_new = BETA_TWO * second + (1.0 - BETA_TWO) * grad * grad
    corr_one = 1.0 - BETA_ONE ** ADAM_STEP
    corr_two = 1.0 - BETA_TWO ** ADAM_STEP
    update = first_new / corr_one / (jnp.sqrt(second_new / corr_two) + EPS_ADAM)
    return (master - rate * (update + decay * master), first_new, second_new)

def reference(tokens_in, cotangent, attention_master, feedforward_master, vector_master, attention_first, attention_second, feedforward_first, feedforward_second, vector_first, vector_second):
    attention = attention_master.astype(jnp.bfloat16)
    feedforward = feedforward_master.astype(jnp.bfloat16)
    vector = vector_master.astype(jnp.bfloat16)

    def one_clip(totals, pair):
        output, grad_tokens, parts = clip_pass(pair[0], pair[1], attention, feedforward, vector)
        summed = (totals[0] + parts[0], totals[1] + parts[1], totals[2] + parts[2])
        return (summed, (output, grad_tokens))
    start = (jnp.zeros(attention_master.shape, jnp.float32), jnp.zeros(feedforward_master.shape, jnp.float32), jnp.zeros(vector_master.shape, jnp.float32))
    totals, (block_out, input_grad) = lax.scan(one_clip, start, (tokens_in, cotangent))
    attention_new, attention_first_new, attention_second_new = adam_update(attention_master, attention_first, attention_second, totals[0], RATE_MATRIX, DECAY_MATRIX)
    feedforward_new, feedforward_first_new, feedforward_second_new = adam_update(feedforward_master, feedforward_first, feedforward_second, totals[1], RATE_MATRIX, DECAY_MATRIX)
    vector_new, vector_first_new, vector_second_new = adam_update(vector_master, vector_first, vector_second, totals[2], RATE_VECTOR, 0.0)
    return (block_out, input_grad, totals[0], totals[1], totals[2], attention_new, feedforward_new, vector_new, attention_first_new, attention_second_new, feedforward_first_new, feedforward_second_new, vector_first_new, vector_second_new)
```

```python
import jax
import jax.numpy as jnp
from jax import lax
from jax.sharding import PartitionSpec as P

D = 768
HEADS = 12
HD = 64
FF = 3072
ADAM_STEP = 2


EPS_NORM = 1e-05
EPS_ADAM = 1e-08
BETA_ONE = 0.9
BETA_TWO = 0.95
RATE_MATRIX = 0.01
RATE_VECTOR = 0.05
DECAY_MATRIX = 0.01


def mix(form, left, right):
    return jnp.einsum(form, left, right, preferred_element_type=jnp.float32)


def times_trans(left, right):
    return lax.dot_general(
        left, right, (((1,), (1,)), ((), ())), preferred_element_type=jnp.float32
    )


def outer_sum(left, right):
    return lax.dot_general(
        left, right, (((0,), (0,)), ((), ())), preferred_element_type=jnp.float32
    )


def layer_norm(field, gain, shift):
    center = field - jnp.mean(field, axis=-1, keepdims=True)
    inverse = lax.rsqrt(jnp.mean(center * center, axis=-1, keepdims=True) + EPS_NORM)
    normed = center * inverse
    return (normed * gain + shift, normed, inverse)


def norm_back(upstream, normed, inverse, gain):
    scaled = upstream * gain
    return inverse * (
        scaled
        - jnp.mean(scaled, axis=-1, keepdims=True)
        - normed * jnp.mean(scaled * normed, axis=-1, keepdims=True)
    )


def gelu_value(pre):
    return 0.5 * pre * (1.0 + lax.erf(pre * 0.7071067811865476))


def gelu_slope(pre):
    return (
        0.5 * (1.0 + lax.erf(pre * 0.7071067811865476))
        + pre * jnp.exp(-0.5 * pre * pre) * 0.3989422804014327
    )


def clip_pass(tokens, upstream, attention, feedforward, vector):
    frames = tokens.shape[0]
    scale = HD ** (-0.5)
    vec = vector.astype(jnp.float32)
    gain_one, shift_one, bias_query, bias_value = vec[0], vec[1], vec[2], vec[3]
    bias_out, gain_two, shift_two, bias_down = vec[4], vec[5], vec[6], vec[7]
    bias_up = jnp.transpose(vec[8:]).reshape(FF)
    w_query = attention[0:D]
    w_key = attention[D : 2 * D]
    w_value = attention[2 * D : 3 * D]
    w_out = attention[3 * D :]
    w_up = feedforward[0:FF]
    w_down = feedforward[FF:]
    normed_out, normed_one, inverse_one = layer_norm(tokens, gain_one, shift_one)
    inputs_bf = normed_out.astype(jnp.bfloat16)
    queries = (
        (times_trans(inputs_bf, w_query) + bias_query)
        .astype(jnp.bfloat16)
        .reshape(frames, HEADS, HD)
    )
    keys_bf = times_trans(inputs_bf, w_key).astype(jnp.bfloat16).reshape(frames, HEADS, HD)
    values_bf = (
        (times_trans(inputs_bf, w_value) + bias_value)
        .astype(jnp.bfloat16)
        .reshape(frames, HEADS, HD)
    )
    scores = mix("qhd,khd->hqk", queries, keys_bf) * scale
    top = jnp.max(scores, axis=-1, keepdims=True)
    lse = top + jnp.log(jnp.sum(jnp.exp(scores - top), axis=-1, keepdims=True))
    weights_bf = jnp.exp(scores - lse).astype(jnp.bfloat16)
    context = mix("hqk,khd->qhd", weights_bf, values_bf).reshape(frames, D).astype(jnp.bfloat16)
    resid = tokens + times_trans(context, w_out) + bias_out
    normed_out_two, normed_two, inverse_two = layer_norm(resid, gain_two, shift_two)
    mlp_in = normed_out_two.astype(jnp.bfloat16)
    pre = times_trans(mlp_in, w_up) + bias_up
    active = gelu_value(pre).astype(jnp.bfloat16)
    output = resid + jnp.dot(active, w_down, preferred_element_type=jnp.float32) + bias_down
    upstream_bf = upstream.astype(jnp.bfloat16)
    grad_bias_down = jnp.sum(upstream, axis=0)
    grad_pre = times_trans(upstream_bf, w_down) * gelu_slope(pre)
    grad_pre_bf = grad_pre.astype(jnp.bfloat16)
    grad_bias_up = jnp.sum(grad_pre, axis=0)
    grad_normed_two = jnp.dot(grad_pre_bf, w_up, preferred_element_type=jnp.float32)
    grad_gain_two = jnp.sum(grad_normed_two * normed_two, axis=0)
    grad_shift_two = jnp.sum(grad_normed_two, axis=0)
    grad_resid = upstream + norm_back(grad_normed_two, normed_two, inverse_two, gain_two)
    resid_bf = grad_resid.astype(jnp.bfloat16)
    grad_bias_out = jnp.sum(grad_resid, axis=0)
    grad_context = jnp.dot(resid_bf, w_out, preferred_element_type=jnp.float32).astype(jnp.bfloat16)
    again = mix("qhd,khd->hqk", queries, keys_bf) * scale
    probs = jnp.exp(again - lse)
    probs_bf = probs.astype(jnp.bfloat16)
    context_heads = grad_context.reshape(frames, HEADS, HD)
    delta = jnp.sum(
        grad_context.astype(jnp.float32).reshape(frames, HEADS, HD)
        * context.astype(jnp.float32).reshape(frames, HEADS, HD),
        axis=-1,
    )
    delta = jnp.transpose(delta)[:, :, None]
    grad_values = mix("hqk,qhd->khd", probs_bf, context_heads).reshape(frames, D)
    grad_probs = mix("qhd,khd->hqk", context_heads, values_bf)
    grad_scores = (probs * (grad_probs - delta)).astype(jnp.bfloat16)
    grad_queries = (mix("hqk,khd->qhd", grad_scores, keys_bf) * scale).reshape(frames, D)
    grad_keys = (mix("hqk,qhd->khd", grad_scores, queries) * scale).reshape(frames, D)
    grad_bias_query = jnp.sum(grad_queries, axis=0)
    grad_bias_value = jnp.sum(grad_values, axis=0)
    queries_grad_bf = grad_queries.astype(jnp.bfloat16)
    keys_grad_bf = grad_keys.astype(jnp.bfloat16)
    values_grad_bf = grad_values.astype(jnp.bfloat16)
    grad_normed_one = (
        jnp.dot(queries_grad_bf, w_query, preferred_element_type=jnp.float32)
        + jnp.dot(keys_grad_bf, w_key, preferred_element_type=jnp.float32)
        + jnp.dot(values_grad_bf, w_value, preferred_element_type=jnp.float32)
    )
    grad_gain_one = jnp.sum(grad_normed_one * normed_one, axis=0)
    grad_shift_one = jnp.sum(grad_normed_one, axis=0)
    grad_tokens = grad_resid + norm_back(grad_normed_one, normed_one, inverse_one, gain_one)
    rows = jnp.stack(
        [
            grad_gain_one,
            grad_shift_one,
            grad_bias_query,
            grad_bias_value,
            grad_bias_out,
            grad_gain_two,
            grad_shift_two,
            grad_bias_down,
        ],
        axis=0,
    )
    up_rows = jnp.transpose(grad_bias_up.reshape(D, FF // D))
    vector_part = jnp.concatenate([rows, up_rows], axis=0)
    attention_pairs = [
        (queries_grad_bf, inputs_bf),
        (keys_grad_bf, inputs_bf),
        (values_grad_bf, inputs_bf),
        (resid_bf, context),
    ]
    feedforward_pairs = [(grad_pre_bf, mlp_in), (active, upstream_bf)]
    return (output, grad_tokens, attention_pairs, feedforward_pairs, vector_part)


def hop(value, bit):
    return lax.ppermute(value, "rep", [(r, r ^ bit) for r in range(8)])


def rounded(value):
    return value.astype(jnp.bfloat16)


def wide(value):
    return value.astype(jnp.float32)


def tree_reduce(keep, give):
    got = hop(give, 1)
    total = rounded(wide(keep) + wide(got))
    got_a = hop(total[:, 1, 0], 2)
    got_b = hop(total[1, :, 1], 4)
    sum_a = rounded(wide(total[:, 0, 0]) + wide(got_a))
    sum_b = rounded(wide(total[0, :, 1]) + wide(got_b))
    last_a = hop(sum_a[1], 4)
    last_b = hop(sum_b[1], 2)
    own = jnp.stack([wide(sum_a[0]) + wide(last_a), wide(sum_b[0]) + wide(last_b)])
    own = rounded(own).reshape(4, -1, D)
    parts = lax.all_to_all(own, "shard", 0, 0)
    return jnp.sum(wide(parts), axis=0)


def reduce_feedforward(pairs, place):
    y, x, c = place
    first = y == 0
    (left_up, right_up), (left_down, right_down) = pairs
    lefts = (jnp.where(first, left_up, left_down), jnp.where(first, left_down, left_up))
    rights = (jnp.where(first, right_up, right_down), jnp.where(first, right_down, right_up))

    def half(c_flip):
        outs = []
        for left, right in zip(lefts, rights):
            blocks = [
                lax.dynamic_slice_in_dim(
                    left, ((x ^ x_flip) * 2 + (c ^ c_flip)) * D, D, axis=1
                )
                for x_flip in range(2)
            ]
            outs.append(rounded(outer_sum(jnp.concatenate(blocks, axis=1), right)))
        return jnp.stack(outs).reshape(2, 2, 2, D // 2, D)

    give = half(1)
    keep = half(0)
    return tree_reduce(keep, give)


def reduce_attention(pairs, place):
    y, x, c = place
    lefts = jnp.stack([left for left, _ in pairs])
    mine = y * 2 + x
    inputs_bf, context = pairs[0][1], pairs[3][1]
    rights = jnp.stack([jnp.where((mine ^ flip) == 3, context, inputs_bf) for flip in range(4)])

    def half(c_flip):
        chosen = jnp.concatenate(
            [
                lax.dynamic_slice(
                    lefts, (mine ^ flip, 0, (c ^ c_flip) * (D // 2)), (1, lefts.shape[1], D // 2)
                )
                for flip in range(4)
            ]
        )
        out = lax.dot_general(
            chosen, rights, (((1,), (1,)), ((0,), (0,))), preferred_element_type=jnp.float32
        )
        return rounded(out).reshape(2, 2, 2, D // 4, D)

    give = half(1)
    keep = half(0)
    return tree_reduce(keep, give)


def reduce_vector(part, tree):
    if not tree:
        return lax.psum(part, ("rep", "shard"))
    for bit in (1, 2, 4):
        part = part + hop(part, bit)
    for bit in (1, 2):
        part = part + lax.ppermute(part, "shard", [(z, z ^ bit) for z in range(4)])
    return part


def adam_update(master, first, second, grad, rate, decay):
    first_new = BETA_ONE * first + (1.0 - BETA_ONE) * grad
    second_new = BETA_TWO * second + (1.0 - BETA_TWO) * grad * grad
    corr_one = 1.0 - BETA_ONE**ADAM_STEP
    corr_two = 1.0 - BETA_TWO**ADAM_STEP
    update = first_new / corr_one / (jnp.sqrt(second_new / corr_two) + EPS_ADAM)
    return (master - rate * (update + decay * master), first_new, second_new)


def body(
    tokens_in,
    cotangent,
    attention_master,
    feedforward_master,
    vector_master,
    attention_first,
    attention_second,
    feedforward_first,
    feedforward_second,
    vector_first,
    vector_second,
):
    attention_own = attention_master.astype(jnp.bfloat16)
    feedforward_own = feedforward_master.astype(jnp.bfloat16)
    vector_own = vector_master.astype(jnp.bfloat16)
    axes = ("rep", "shard")
    rows = attention_master.shape[0]
    features = vector_master.shape[0] // 12
    vector_rows = jnp.pad(
        jnp.transpose(vector_own.reshape(features, 12)), ((0, 4), (0, D - features))
    )
    packed = lax.all_gather(jnp.concatenate([attention_own, vector_rows]), axes, axis=0)
    feedforward = lax.all_gather(feedforward_own, axes, axis=0, tiled=True)
    attention = packed[:, :rows].reshape(4 * D, D)
    vector = jnp.transpose(packed[:, rows : rows + 12, :features], (1, 0, 2)).reshape(12, D)
    output, grad_tokens, attention_pairs, feedforward_pairs, vector_part = clip_pass(
        tokens_in[0], cotangent[0], attention, feedforward, vector
    )
    block_out = output[None]
    input_grad = grad_tokens[None]
    rep, shard = lax.axis_size("rep"), lax.axis_size("shard")
    tree = rep == 8 and shard == 4
    if tree:
        spot = lax.axis_index("rep")
        place = (spot // 4, (spot // 2) % 2, spot % 2)
        feedforward_grad = reduce_feedforward(feedforward_pairs, place)
        attention_grad = reduce_attention(attention_pairs, place)
    else:
        feedforward_grad, attention_grad = [
            wide(
                lax.psum_scatter(
                    rounded(jnp.concatenate([outer_sum(*pair) for pair in pairs])),
                    axes,
                    scatter_dimension=0,
                    tiled=True,
                )
            )
            for pairs in (feedforward_pairs, attention_pairs)
        ]
    vector_sum = reduce_vector(vector_part, tree)
    owner = lax.axis_index("rep") * shard + lax.axis_index("shard")
    vector_grad = jnp.transpose(
        lax.dynamic_slice_in_dim(vector_sum, owner * features, features, axis=1)
    ).reshape(-1)
    attention_new, attention_first_new, attention_second_new = adam_update(
        attention_master,
        attention_first,
        attention_second,
        attention_grad,
        RATE_MATRIX,
        DECAY_MATRIX,
    )
    feedforward_new, feedforward_first_new, feedforward_second_new = adam_update(
        feedforward_master,
        feedforward_first,
        feedforward_second,
        feedforward_grad,
        RATE_MATRIX,
        DECAY_MATRIX,
    )
    vector_new, vector_first_new, vector_second_new = adam_update(
        vector_master, vector_first, vector_second, vector_grad, RATE_VECTOR, 0.0
    )
    return (
        block_out,
        input_grad,
        attention_grad,
        feedforward_grad,
        vector_grad,
        attention_new,
        feedforward_new,
        vector_new,
        attention_first_new,
        attention_second_new,
        feedforward_first_new,
        feedforward_second_new,
        vector_first_new,
        vector_second_new,
    )


def solution(mesh):
    placed = (
        P(("rep", "shard"), None, None),
        P(("rep", "shard"), None, None),
        P(("rep", "shard"), None),
        P(("rep", "shard"), None),
        P(("rep", "shard")),
        P(("rep", "shard"), None),
        P(("rep", "shard"), None),
        P(("rep", "shard"), None),
        P(("rep", "shard"), None),
        P(("rep", "shard")),
        P(("rep", "shard")),
    )
    return jax.shard_map(
        body,
        mesh=mesh,
        in_specs=placed,
        out_specs=(
            P(("rep", "shard"), None, None),
            P(("rep", "shard"), None, None),
            P(("rep", "shard"), None),
            P(("rep", "shard"), None),
            P(("rep", "shard")),
            P(("rep", "shard"), None),
            P(("rep", "shard"), None),
            P(("rep", "shard")),
            P(("rep", "shard"), None),
            P(("rep", "shard"), None),
            P(("rep", "shard"), None),
            P(("rep", "shard"), None),
            P(("rep", "shard")),
            P(("rep", "shard")),
        ),
        check_vma=False,
    )
```

```python
import jax
import jax.numpy as jnp
from jax import lax
from jax.experimental import pallas as pl
from jax.experimental.pallas import tpu as pltpu
from jax.sharding import PartitionSpec as P

D = 768
HEADS = 12
HD = 64
FF = 3072
ADAM_STEP = 2


EPS_NORM = 1e-05
EPS_ADAM = 1e-08
BETA_ONE = 0.9
BETA_TWO = 0.95
RATE_MATRIX = 0.01
RATE_VECTOR = 0.05
DECAY_MATRIX = 0.01


def mix(form, left, right):
    return jnp.einsum(form, left, right, preferred_element_type=jnp.float32)


def times_trans(left, right):
    return lax.dot_general(
        left, right, (((1,), (1,)), ((), ())), preferred_element_type=jnp.float32
    )


def outer_sum(left, right):
    return lax.dot_general(
        left, right, (((0,), (0,)), ((), ())), preferred_element_type=jnp.float32
    )


def layer_norm(field, gain, shift):
    center = field - jnp.mean(field, axis=-1, keepdims=True)
    inverse = lax.rsqrt(jnp.mean(center * center, axis=-1, keepdims=True) + EPS_NORM)
    normed = center * inverse
    return (normed * gain + shift, normed, inverse)


def norm_back(upstream, normed, inverse, gain):
    scaled = upstream * gain
    return inverse * (
        scaled
        - jnp.mean(scaled, axis=-1, keepdims=True)
        - normed * jnp.mean(scaled * normed, axis=-1, keepdims=True)
    )


def gelu_value(pre):
    return 0.5 * pre * (1.0 + lax.erf(pre * 0.7071067811865476))


def gelu_slope(pre):
    return (
        0.5 * (1.0 + lax.erf(pre * 0.7071067811865476))
        + pre * jnp.exp(-0.5 * pre * pre) * 0.3989422804014327
    )


def clip_pass(tokens, upstream, attention, feedforward, vector, place):
    frames = tokens.shape[0]
    scale = HD ** (-0.5)
    vec = vector.astype(jnp.float32)
    gain_one, shift_one, bias_query, bias_value = vec[0], vec[1], vec[2], vec[3]
    bias_out, gain_two, shift_two, bias_down = vec[4], vec[5], vec[6], vec[7]
    bias_up = jnp.transpose(vec[8:]).reshape(FF)
    w_query, w_key, w_value, w_out = attention
    w_up, w_down = feedforward
    normed_out, normed_one, inverse_one = layer_norm(tokens, gain_one, shift_one)
    inputs_bf = normed_out.astype(jnp.bfloat16)
    queries = (
        (times_trans(inputs_bf, w_query) + bias_query)
        .astype(jnp.bfloat16)
        .reshape(frames, HEADS, HD)
    )
    keys_bf = times_trans(inputs_bf, w_key).astype(jnp.bfloat16).reshape(frames, HEADS, HD)
    values_bf = (
        (times_trans(inputs_bf, w_value) + bias_value)
        .astype(jnp.bfloat16)
        .reshape(frames, HEADS, HD)
    )
    scores = mix("qhd,khd->hqk", queries, keys_bf) * scale
    top = jnp.max(scores, axis=-1, keepdims=True)
    lse = top + jnp.log(jnp.sum(jnp.exp(scores - top), axis=-1, keepdims=True))
    weights_bf = jnp.exp(scores - lse).astype(jnp.bfloat16)
    context = mix("hqk,khd->qhd", weights_bf, values_bf).reshape(frames, D).astype(jnp.bfloat16)
    resid = tokens + times_trans(context, w_out) + bias_out
    normed_out_two, normed_two, inverse_two = layer_norm(resid, gain_two, shift_two)
    mlp_in = normed_out_two.astype(jnp.bfloat16)
    pre = times_trans(mlp_in, w_up) + bias_up
    active = gelu_value(pre).astype(jnp.bfloat16)
    output = resid + jnp.dot(active, w_down, preferred_element_type=jnp.float32) + bias_down
    upstream_bf = upstream.astype(jnp.bfloat16)
    grad_bias_down = jnp.sum(upstream, axis=0)
    grad_pre = times_trans(upstream_bf, w_down) * gelu_slope(pre)
    grad_pre_bf = grad_pre.astype(jnp.bfloat16)
    grad_bias_up = jnp.sum(grad_pre, axis=0)
    tree = place is not None
    feedforward_pairs = [(grad_pre_bf, mlp_in), (active, upstream_bf)]
    feedforward_grad = attention_grad = None
    if tree:
        keep, give = split_feedforward(feedforward_pairs, place)
        keep, give, grad_pre_bf = lax.optimization_barrier((keep, give, grad_pre_bf))
        got = hop(give, 1)
    grad_normed_two = jnp.dot(grad_pre_bf, w_up, preferred_element_type=jnp.float32)
    grad_gain_two = jnp.sum(grad_normed_two * normed_two, axis=0)
    grad_shift_two = jnp.sum(grad_normed_two, axis=0)
    grad_resid = upstream + norm_back(grad_normed_two, normed_two, inverse_two, gain_two)
    resid_bf = grad_resid.astype(jnp.bfloat16)
    grad_bias_out = jnp.sum(grad_resid, axis=0)
    grad_context = jnp.dot(resid_bf, w_out, preferred_element_type=jnp.float32).astype(jnp.bfloat16)
    if tree:
        got, resid_bf, grad_context = lax.optimization_barrier((got, resid_bf, grad_context))
        total = rounded(wide(keep) + wide(got))
        total, grad_context = lax.optimization_barrier((total, grad_context))
        got_a, got_b = tree_middle(total)
    again = mix("qhd,khd->hqk", queries, keys_bf) * scale
    probs = jnp.exp(again - lse)
    probs_bf = probs.astype(jnp.bfloat16)
    context_heads = grad_context.reshape(frames, HEADS, HD)
    delta = jnp.sum(
        grad_context.astype(jnp.float32).reshape(frames, HEADS, HD)
        * context.astype(jnp.float32).reshape(frames, HEADS, HD),
        axis=-1,
    )
    delta = jnp.transpose(delta)[:, :, None]
    grad_values = mix("hqk,qhd->khd", probs_bf, context_heads).reshape(frames, D)
    grad_probs = mix("qhd,khd->hqk", context_heads, values_bf)
    grad_scores = (probs * (grad_probs - delta)).astype(jnp.bfloat16)
    grad_queries = (mix("hqk,khd->qhd", grad_scores, keys_bf) * scale).reshape(frames, D)
    grad_keys = (mix("hqk,qhd->khd", grad_scores, queries) * scale).reshape(frames, D)
    grad_bias_query = jnp.sum(grad_queries, axis=0)
    grad_bias_value = jnp.sum(grad_values, axis=0)
    queries_grad_bf = grad_queries.astype(jnp.bfloat16)
    keys_grad_bf = grad_keys.astype(jnp.bfloat16)
    values_grad_bf = grad_values.astype(jnp.bfloat16)
    attention_pairs = [
        (queries_grad_bf, inputs_bf),
        (keys_grad_bf, inputs_bf),
        (values_grad_bf, inputs_bf),
        (resid_bf, context),
    ]
    if tree:
        keep, give = split_attention(attention_pairs, place)
        keep, give, got_a, got_b = lax.optimization_barrier((keep, give, got_a, got_b))
        got = hop(give, 1)
        sums = tree_sums(total, got_a, got_b)
        lasts = tree_last(sums)
        sums, queries_grad_bf, got = lax.optimization_barrier((sums, queries_grad_bf, got))
        total = rounded(wide(keep) + wide(got))
        got_a, got_b = tree_middle(total)
        total, queries_grad_bf = lax.optimization_barrier((total, queries_grad_bf))
        got_a, got_b, lasts = lax.optimization_barrier((got_a, got_b, lasts))
        feedforward_own = tree_own(sums, lasts)
    grad_normed_one = (
        jnp.dot(queries_grad_bf, w_query, preferred_element_type=jnp.float32)
        + jnp.dot(keys_grad_bf, w_key, preferred_element_type=jnp.float32)
        + jnp.dot(values_grad_bf, w_value, preferred_element_type=jnp.float32)
    )
    grad_gain_one = jnp.sum(grad_normed_one * normed_one, axis=0)
    grad_shift_one = jnp.sum(grad_normed_one, axis=0)
    grad_tokens = grad_resid + norm_back(grad_normed_one, normed_one, inverse_one, gain_one)
    rows = jnp.stack(
        [
            grad_gain_one,
            grad_shift_one,
            grad_bias_query,
            grad_bias_value,
            grad_bias_out,
            grad_gain_two,
            grad_shift_two,
            grad_bias_down,
        ],
        axis=0,
    )
    up_rows = jnp.transpose(grad_bias_up.reshape(D, FF // D))
    vector_part = jnp.concatenate([rows, up_rows], axis=0)
    if tree:
        feedforward_grad = tree_finish(feedforward_own)
        sums = tree_sums(total, got_a, got_b)
        attention_grad = tree_finish(tree_own(sums, tree_last(sums)))
    else:
        feedforward_grad, attention_grad = [
            wide(
                lax.psum_scatter(
                    rounded(jnp.concatenate([outer_sum(*pair) for pair in pairs])),
                    ("rep", "shard"),
                    scatter_dimension=0,
                    tiled=True,
                )
            )
            for pairs in (feedforward_pairs, attention_pairs)
        ]
    return (output, grad_tokens, attention_grad, feedforward_grad, vector_part)


def hop(value, bit):
    return lax.ppermute(value, "rep", [(r, r ^ bit) for r in range(8)])


def rounded(value):
    return value.astype(jnp.bfloat16)


def wide(value):
    return value.astype(jnp.float32)


def tree_middle(total):
    return hop(total[:, 1, 0], 2), hop(total[1, :, 1], 4)


def tree_sums(total, got_a, got_b):
    sum_a = rounded(wide(total[:, 0, 0]) + wide(got_a))
    sum_b = rounded(wide(total[0, :, 1]) + wide(got_b))
    return sum_a, sum_b


def tree_last(sums):
    return hop(sums[0][1], 4), hop(sums[1][1], 2)


def tree_own(sums, lasts):
    own = jnp.stack([wide(part[0]) + wide(last) for part, last in zip(sums, lasts)])
    return rounded(own).reshape(4, -1, D)


def tree_finish(own):
    return jnp.sum(wide(lax.all_to_all(own, "shard", 0, 0)), axis=0)


FLIPS = ((0, 0, 0, 4), (0, 1, 0, 4), (1, 0, 0, 4), (1, 1, 0, 2), (1, 1, 2, 4))


def assemble(pieces, splits, place):
    y, x, c = place
    count = len(pieces) * len(splits)
    spots = jnp.stack(
        [
            ((y ^ y_flip) * 2 + (x ^ x_flip)) * 2 + (c ^ c_flip)
            for c_flip in range(2)
            for y_flip, x_flip, _, _ in FLIPS
        ]
    ).astype(jnp.int32)

    def kernel(spots_ref, *refs):
        ins, outs, sems = refs[: len(pieces)], refs[len(pieces) : -1], refs[-1]

        def copy_of(at, part, group):
            _, _, low, high = FLIPS[at % len(FLIPS)]
            rows, groups = splits[part]
            first = sum(many for _, many in splits[:part])
            return pltpu.make_async_copy(
                ins[at].at[:, pl.ds(sum(many for many, _ in splits[:part]), rows)],
                outs[first + group].at[spots_ref[at] % (8 // groups), pl.ds(low, high - low)],
                sems.at[at * len(splits) + part],
            )

        jobs = [(at, part) for at in range(len(pieces)) for part in range(len(splits))]
        for at, part in jobs:
            groups = splits[part][1]
            for group in range(groups):

                @pl.when(spots_ref[at] // (8 // groups) == group)
                def _():
                    copy_of(at, part, group).start()

        for at, part in jobs:
            copy_of(at, part, 0).wait()

    return pl.pallas_call(
        kernel,
        out_shape=[
            jax.ShapeDtypeStruct((8 // groups, 4, rows, D), jnp.bfloat16)
            for rows, groups in splits
            for _ in range(groups)
        ],
        in_specs=[pl.BlockSpec(memory_space=pltpu.SMEM)]
        + [pl.BlockSpec(memory_space=pl.ANY)] * len(pieces),
        out_specs=[pl.BlockSpec(memory_space=pltpu.VMEM)] * sum(groups for _, groups in splits),
        scratch_shapes=[pltpu.SemaphoreType.DMA((count,))],
        compiler_params=pltpu.CompilerParams(vmem_limit_bytes=24 * 1024 * 1024),
    )(spots, *pieces)


def tree_gather(column, splits, place):
    by_x, by_y = hop(column, 2), hop(column, 4)
    mine = [column, by_x, by_y, hop(by_y[:2], 2), hop(by_x[2:], 4)]
    theirs = [hop(part, 1) for part in mine]
    return assemble(mine + theirs, splits, place)


def split_feedforward(pairs, place):
    y, x, c = place
    first = y == 0
    (left_up, right_up), (left_down, right_down) = pairs
    lefts = (jnp.where(first, left_up, left_down), jnp.where(first, left_down, left_up))
    rights = (jnp.where(first, right_up, right_down), jnp.where(first, right_down, right_up))

    def half(c_flip):
        outs = []
        for left, right in zip(lefts, rights):
            blocks = [
                lax.dynamic_slice_in_dim(
                    left, ((x ^ x_flip) * 2 + (c ^ c_flip)) * D, D, axis=1
                )
                for x_flip in range(2)
            ]
            outs.append(rounded(outer_sum(jnp.concatenate(blocks, axis=1), right)))
        return jnp.stack(outs).reshape(2, 2, 2, D // 2, D)

    give = half(1)
    keep = half(0)
    return keep, give


def split_attention(pairs, place):
    y, x, c = place
    lefts = jnp.stack([left for left, _ in pairs])
    mine = y * 2 + x
    inputs_bf, context = pairs[0][1], pairs[3][1]
    rights = jnp.stack([jnp.where((mine ^ flip) == 3, context, inputs_bf) for flip in range(4)])

    def half(c_flip):
        chosen = jnp.concatenate(
            [
                lax.dynamic_slice(
                    lefts, (mine ^ flip, 0, (c ^ c_flip) * (D // 2)), (1, lefts.shape[1], D // 2)
                )
                for flip in range(4)
            ]
        )
        out = lax.dot_general(
            chosen, rights, (((1,), (1,)), ((0,), (0,))), preferred_element_type=jnp.float32
        )
        return rounded(out).reshape(2, 2, 2, D // 4, D)

    give = half(1)
    keep = half(0)
    return keep, give


def reduce_vector(part, tree):
    if not tree:
        return lax.psum(part, ("rep", "shard"))
    for bit in (1, 2, 4):
        part = part + hop(part, bit)
    for bit in (1, 2):
        part = part + lax.ppermute(part, "shard", [(z, z ^ bit) for z in range(4)])
    return part


def adam_update(master, first, second, grad, rate, decay):
    first_new = BETA_ONE * first + (1.0 - BETA_ONE) * grad
    second_new = BETA_TWO * second + (1.0 - BETA_TWO) * grad * grad
    corr_one = 1.0 - BETA_ONE**ADAM_STEP
    corr_two = 1.0 - BETA_TWO**ADAM_STEP
    update = first_new / corr_one / (jnp.sqrt(second_new / corr_two) + EPS_ADAM)
    return (master - rate * (update + decay * master), first_new, second_new)


def body(
    tokens_in,
    cotangent,
    attention_master,
    feedforward_master,
    vector_master,
    attention_first,
    attention_second,
    feedforward_first,
    feedforward_second,
    vector_first,
    vector_second,
):
    attention_own = attention_master.astype(jnp.bfloat16)
    feedforward_own = feedforward_master.astype(jnp.bfloat16)
    vector_own = vector_master.astype(jnp.bfloat16)
    axes = ("rep", "shard")
    rows = attention_master.shape[0]
    features = vector_master.shape[0] // 12
    vector_rows = jnp.pad(
        jnp.transpose(vector_own.reshape(features, 12)), ((0, 4), (0, D - features))
    )
    packed = jnp.concatenate([attention_own, vector_rows])
    rep, shard = lax.axis_size("rep"), lax.axis_size("shard")
    tree = rep == 8 and shard == 4
    place = None
    if tree:
        spot = lax.axis_index("rep")
        place = (spot // 4, (spot // 2) % 2, spot % 2)
        column = lax.all_gather(packed, "shard", axis=0)
        wide_column = lax.all_gather(feedforward_own, "shard", axis=0)
        *attention, vector = tree_gather(column, ((rows, 4), (16, 1)), place)
        feedforward = tree_gather(wide_column, ((feedforward_own.shape[0], 2),), place)
        attention = [part.reshape(D, D) for part in attention]
        feedforward = [part.reshape(FF, D) for part in feedforward]
        vector = vector.reshape(32, 16, D)[:, :12, :features]
    else:
        packed = lax.all_gather(packed, axes, axis=0)
        feedforward = lax.all_gather(feedforward_own, axes, axis=0, tiled=True)
        attention = jnp.split(packed[:, :rows].reshape(4 * D, D), 4)
        feedforward = jnp.split(feedforward, 2)
        vector = packed[:, rows : rows + 12, :features]
    vector = jnp.transpose(vector, (1, 0, 2)).reshape(12, D)
    output, grad_tokens, attention_grad, feedforward_grad, vector_part = clip_pass(
        tokens_in[0], cotangent[0], attention, feedforward, vector, place
    )
    block_out = output[None]
    input_grad = grad_tokens[None]
    vector_sum = reduce_vector(vector_part, tree)
    owner = lax.axis_index("rep") * shard + lax.axis_index("shard")
    vector_grad = jnp.transpose(
        lax.dynamic_slice_in_dim(vector_sum, owner * features, features, axis=1)
    ).reshape(-1)
    attention_new, attention_first_new, attention_second_new = adam_update(
        attention_master,
        attention_first,
        attention_second,
        attention_grad,
        RATE_MATRIX,
        DECAY_MATRIX,
    )
    feedforward_new, feedforward_first_new, feedforward_second_new = adam_update(
        feedforward_master,
        feedforward_first,
        feedforward_second,
        feedforward_grad,
        RATE_MATRIX,
        DECAY_MATRIX,
    )
    vector_new, vector_first_new, vector_second_new = adam_update(
        vector_master, vector_first, vector_second, vector_grad, RATE_VECTOR, 0.0
    )
    return (
        block_out,
        input_grad,
        attention_grad,
        feedforward_grad,
        vector_grad,
        attention_new,
        feedforward_new,
        vector_new,
        attention_first_new,
        attention_second_new,
        feedforward_first_new,
        feedforward_second_new,
        vector_first_new,
        vector_second_new,
    )


def solution(mesh):
    placed = (
        P(("rep", "shard"), None, None),
        P(("rep", "shard"), None, None),
        P(("rep", "shard"), None),
        P(("rep", "shard"), None),
        P(("rep", "shard")),
        P(("rep", "shard"), None),
        P(("rep", "shard"), None),
        P(("rep", "shard"), None),
        P(("rep", "shard"), None),
        P(("rep", "shard")),
        P(("rep", "shard")),
    )
    return jax.shard_map(
        body,
        mesh=mesh,
        in_specs=placed,
        out_specs=(
            P(("rep", "shard"), None, None),
            P(("rep", "shard"), None, None),
            P(("rep", "shard"), None),
            P(("rep", "shard"), None),
            P(("rep", "shard")),
            P(("rep", "shard"), None),
            P(("rep", "shard"), None),
            P(("rep", "shard")),
            P(("rep", "shard"), None),
            P(("rep", "shard"), None),
            P(("rep", "shard"), None),
            P(("rep", "shard"), None),
            P(("rep", "shard")),
            P(("rep", "shard")),
        ),
        check_vma=False,
    )
```

```python
import jax
import jax.numpy as jnp
from jax import lax
from jax.experimental import pallas as pl
from jax.experimental.pallas import tpu as pltpu
from jax.sharding import PartitionSpec as P

D = 768
HEADS = 12
HD = 64
FF = 3072
ADAM_STEP = 2


EPS_NORM = 1e-05
EPS_ADAM = 1e-08
BETA_ONE = 0.9
BETA_TWO = 0.95
RATE_MATRIX = 0.01
RATE_VECTOR = 0.05
DECAY_MATRIX = 0.01


def mix(form, left, right):
    return jnp.einsum(form, left, right, preferred_element_type=jnp.float32)


def times_trans(left, right):
    return lax.dot_general(
        left, right, (((1,), (1,)), ((), ())), preferred_element_type=jnp.float32
    )


def outer_sum(left, right):
    return lax.dot_general(
        left, right, (((0,), (0,)), ((), ())), preferred_element_type=jnp.float32
    )


def layer_norm(field, gain, shift):
    center = field - jnp.mean(field, axis=-1, keepdims=True)
    inverse = lax.rsqrt(jnp.mean(center * center, axis=-1, keepdims=True) + EPS_NORM)
    normed = center * inverse
    return (normed * gain + shift, normed, inverse)


def norm_back(upstream, normed, inverse, gain):
    scaled = upstream * gain
    return inverse * (
        scaled
        - jnp.mean(scaled, axis=-1, keepdims=True)
        - normed * jnp.mean(scaled * normed, axis=-1, keepdims=True)
    )


def gelu_value(pre):
    return 0.5 * pre * (1.0 + lax.erf(pre * 0.7071067811865476))


def gelu_slope(pre):
    return (
        0.5 * (1.0 + lax.erf(pre * 0.7071067811865476))
        + pre * jnp.exp(-0.5 * pre * pre) * 0.3989422804014327
    )


def clip_pass(tokens, upstream, attention, feedforward, vec, bias_up, place):
    frames = tokens.shape[0]
    scale = HD ** (-0.5)
    gain_one, shift_one, bias_query, bias_value = vec[0], vec[1], vec[2], vec[3]
    bias_out, gain_two, shift_two, bias_down = vec[4], vec[5], vec[6], vec[7]
    w_query, w_key, w_value, w_out = attention
    w_up, w_down = feedforward
    normed_out, normed_one, inverse_one = layer_norm(tokens, gain_one, shift_one)
    inputs_bf = normed_out.astype(jnp.bfloat16)
    queries = (
        (times_trans(inputs_bf, w_query) + bias_query)
        .astype(jnp.bfloat16)
        .reshape(frames, HEADS, HD)
    )
    keys_bf = times_trans(inputs_bf, w_key).astype(jnp.bfloat16).reshape(frames, HEADS, HD)
    values_bf = (
        (times_trans(inputs_bf, w_value) + bias_value)
        .astype(jnp.bfloat16)
        .reshape(frames, HEADS, HD)
    )
    scores = mix("qhd,khd->hqk", queries, keys_bf) * scale
    top = jnp.max(scores, axis=-1, keepdims=True)
    lse = top + jnp.log(jnp.sum(jnp.exp(scores - top), axis=-1, keepdims=True))
    weights_bf = jnp.exp(scores - lse).astype(jnp.bfloat16)
    context = mix("hqk,khd->qhd", weights_bf, values_bf).reshape(frames, D).astype(jnp.bfloat16)
    resid = tokens + times_trans(context, w_out) + bias_out
    normed_out_two, normed_two, inverse_two = layer_norm(resid, gain_two, shift_two)
    mlp_in = normed_out_two.astype(jnp.bfloat16)
    pre = times_trans(mlp_in, w_up) + bias_up
    active = gelu_value(pre).astype(jnp.bfloat16)
    output = resid + jnp.dot(active, w_down, preferred_element_type=jnp.float32) + bias_down
    upstream_bf = upstream.astype(jnp.bfloat16)
    grad_bias_down = jnp.sum(upstream, axis=0)
    grad_pre = times_trans(upstream_bf, w_down) * gelu_slope(pre)
    grad_pre_bf = grad_pre.astype(jnp.bfloat16)
    grad_bias_up = jnp.sum(grad_pre, axis=0)
    tree = place is not None
    feedforward_pairs = [(grad_pre_bf, mlp_in), (active, upstream_bf)]
    feedforward_grad = attention_grad = None
    if tree:
        keep, give = split_feedforward(feedforward_pairs, place)
        keep, give, grad_pre_bf = lax.optimization_barrier((keep, give, grad_pre_bf))
        got = hop(give, 1)
    grad_normed_two = jnp.dot(grad_pre_bf, w_up, preferred_element_type=jnp.float32)
    grad_gain_two = jnp.sum(grad_normed_two * normed_two, axis=0)
    grad_shift_two = jnp.sum(grad_normed_two, axis=0)
    grad_resid = upstream + norm_back(grad_normed_two, normed_two, inverse_two, gain_two)
    resid_bf = grad_resid.astype(jnp.bfloat16)
    grad_bias_out = jnp.sum(grad_resid, axis=0)
    grad_context = jnp.dot(resid_bf, w_out, preferred_element_type=jnp.float32).astype(jnp.bfloat16)
    if tree:
        got, resid_bf, grad_context = lax.optimization_barrier((got, resid_bf, grad_context))
        total = rounded(wide(keep) + wide(got))
        total, grad_context = lax.optimization_barrier((total, grad_context))
        got_a, got_b = tree_middle(total)
    again = mix("qhd,khd->hqk", queries, keys_bf) * scale
    probs = jnp.exp(again - lse)
    probs_bf = probs.astype(jnp.bfloat16)
    context_heads = grad_context.reshape(frames, HEADS, HD)
    delta = jnp.sum(
        grad_context.astype(jnp.float32).reshape(frames, HEADS, HD)
        * context.astype(jnp.float32).reshape(frames, HEADS, HD),
        axis=-1,
    )
    delta = jnp.transpose(delta)[:, :, None]
    grad_values = mix("hqk,qhd->khd", probs_bf, context_heads).reshape(frames, D)
    grad_probs = mix("qhd,khd->hqk", context_heads, values_bf)
    grad_scores = (probs * (grad_probs - delta)).astype(jnp.bfloat16)
    grad_queries = (mix("hqk,khd->qhd", grad_scores, keys_bf) * scale).reshape(frames, D)
    grad_keys = (mix("hqk,qhd->khd", grad_scores, queries) * scale).reshape(frames, D)
    grad_bias_query = jnp.sum(grad_queries, axis=0)
    grad_bias_value = jnp.sum(grad_values, axis=0)
    queries_grad_bf = grad_queries.astype(jnp.bfloat16)
    keys_grad_bf = grad_keys.astype(jnp.bfloat16)
    values_grad_bf = grad_values.astype(jnp.bfloat16)
    attention_pairs = [
        (queries_grad_bf, inputs_bf),
        (keys_grad_bf, inputs_bf),
        (values_grad_bf, inputs_bf),
        (resid_bf, context),
    ]
    if tree:
        keep, give = split_attention(attention_pairs, place)
        keep, give, got_a, got_b, output = lax.optimization_barrier(
            (keep, give, got_a, got_b, output)
        )
        got = hop(give, 1)
        sums = tree_sums(total, got_a, got_b)
        lasts = tree_last(sums)
        sums, queries_grad_bf, got = lax.optimization_barrier((sums, queries_grad_bf, got))
        total = rounded(wide(keep) + wide(got))
        got_a, got_b = tree_middle(total)
        total, queries_grad_bf = lax.optimization_barrier((total, queries_grad_bf))
    grad_normed_one = (
        jnp.dot(queries_grad_bf, w_query, preferred_element_type=jnp.float32)
        + jnp.dot(keys_grad_bf, w_key, preferred_element_type=jnp.float32)
        + jnp.dot(values_grad_bf, w_value, preferred_element_type=jnp.float32)
    )
    grad_gain_one = jnp.sum(grad_normed_one * normed_one, axis=0)
    grad_shift_one = jnp.sum(grad_normed_one, axis=0)
    grad_tokens = grad_resid + norm_back(grad_normed_one, normed_one, inverse_one, gain_one)
    rows = jnp.stack(
        [
            grad_gain_one,
            grad_shift_one,
            grad_bias_query,
            grad_bias_value,
            grad_bias_out,
            grad_gain_two,
            grad_shift_two,
            grad_bias_down,
        ],
        axis=0,
    )
    vector_part = jnp.concatenate([rows, grad_bias_up.reshape(FF // D, D)], axis=0)
    if tree:
        got_a, got_b, lasts, vector_part, grad_tokens = lax.optimization_barrier(
            (got_a, got_b, lasts, vector_part, grad_tokens)
        )
        blocks = tree_blocks(tree_own(sums, lasts))
        blocks, got_a, got_b, vector_part = lax.optimization_barrier(
            (blocks, got_a, got_b, vector_part)
        )
        feedforward_parts = tree_column(blocks)
        sums = tree_sums(total, got_a, got_b)
        lasts = tree_last(sums)
        vector_part = vector_part + sum(hop(vector_part, flip) for flip in range(1, 8))
        lasts, feedforward_parts, vector_part = lax.optimization_barrier(
            (lasts, feedforward_parts, vector_part)
        )
        attention_parts = tree_column(tree_blocks(tree_own(sums, lasts)))
        vector_sum = vector_part + sum(turn(vector_part, step) for step in range(1, 4))
        feedforward_grad = sum(wide(part) for part in feedforward_parts)
        attention_grad = sum(wide(part) for part in attention_parts)
    else:
        feedforward_grad, attention_grad = [
            wide(
                lax.psum_scatter(
                    rounded(jnp.concatenate([outer_sum(*pair) for pair in pairs])),
                    ("rep", "shard"),
                    scatter_dimension=0,
                    tiled=True,
                )
            )
            for pairs in (feedforward_pairs, attention_pairs)
        ]
        vector_sum = lax.psum(vector_part, ("rep", "shard"))
    return (output, grad_tokens, attention_grad, feedforward_grad, vector_sum)


def hop(value, bit):
    return lax.ppermute(value, "rep", [(r, r ^ bit) for r in range(8)])


def rounded(value):
    return value.astype(jnp.bfloat16)


def wide(value):
    return value.astype(jnp.float32)


def tree_middle(total):
    return hop(total[:, 1, 0], 2), hop(total[1, :, 1], 4)


def tree_sums(total, got_a, got_b):
    sum_a = rounded(wide(total[:, 0, 0]) + wide(got_a))
    sum_b = rounded(wide(total[0, :, 1]) + wide(got_b))
    return sum_a, sum_b


def tree_last(sums):
    return hop(sums[0][1], 4), hop(sums[1][1], 2)


def tree_own(sums, lasts):
    own = jnp.stack([wide(part[0]) + wide(last) for part, last in zip(sums, lasts)])
    return rounded(own).reshape(4, -1, D)


def turn(value, step):
    return lax.ppermute(value, "shard", [(z, (z + step) % 4) for z in range(4)])


def tree_blocks(own):
    z = lax.axis_index("shard")
    return [lax.dynamic_index_in_dim(own, (z + 4 - k) % 4, 0, False) for k in range(4)]


def tree_column(blocks):
    return [blocks[0]] + [turn(blocks[k], -k) for k in range(1, 4)]


FLIPS = ((0, 0, 0, 4), (0, 1, 0, 4), (1, 0, 0, 4), (1, 1, 0, 2), (1, 1, 2, 4))


def assemble(pieces, splits, place):
    y, x, c = place
    z = lax.axis_index("shard")
    counts = [high - low for _, _, low, high in FLIPS] * 2
    count = sum(counts) * len(splits)
    spots = jnp.stack(
        [
            ((y ^ y_flip) * 2 + (x ^ x_flip)) * 2 + (c ^ c_flip)
            for c_flip in range(2)
            for y_flip, x_flip, _, _ in FLIPS
        ]
        + [(z + 4 - k) % 4 for k in range(4)]
    ).astype(jnp.int32)

    def kernel(spots_ref, *refs):
        ins, outs, sems = refs[: len(pieces)], refs[len(pieces) : -1], refs[-1]

        def copy_of(at, block, part, group):
            low = FLIPS[at % len(FLIPS)][2]
            rows, groups = splits[part]
            first = sum(many for _, many in splits[:part])
            return pltpu.make_async_copy(
                ins[at].at[block, pl.ds(sum(many for many, _ in splits[:part]), rows)],
                outs[first + group].at[
                    spots_ref[at] % (8 // groups), spots_ref[len(pieces) + low + block]
                ],
                sems.at[(sum(counts[:at]) + block) * len(splits) + part],
            )

        jobs = [
            (at, block, part)
            for at in range(len(pieces))
            for block in range(counts[at])
            for part in range(len(splits))
        ]
        for at, block, part in jobs:
            groups = splits[part][1]
            for group in range(groups):

                @pl.when(spots_ref[at] // (8 // groups) == group)
                def _():
                    copy_of(at, block, part, group).start()

        for at, block, part in jobs:
            copy_of(at, block, part, 0).wait()

    return pl.pallas_call(
        kernel,
        out_shape=[
            jax.ShapeDtypeStruct((8 // groups, 4, rows, D), jnp.bfloat16)
            for rows, groups in splits
            for _ in range(groups)
        ],
        in_specs=[pl.BlockSpec(memory_space=pltpu.SMEM)]
        + [pl.BlockSpec(memory_space=pl.ANY)] * len(pieces),
        out_specs=[pl.BlockSpec(memory_space=pltpu.VMEM)] * sum(groups for _, groups in splits),
        scratch_shapes=[pltpu.SemaphoreType.DMA((count,))],
        compiler_params=pltpu.CompilerParams(vmem_limit_bytes=24 * 1024 * 1024),
    )(spots, *pieces)


def tree_sides(column):
    column = jnp.stack(column)
    return [column, hop(column, 2), hop(column, 4)]


def tree_gather(mine, splits, place):
    _, by_x, by_y = mine
    mine = mine + [hop(by_y[:2], 2), hop(by_x[2:], 4)]
    theirs = [hop(part, 1) for part in mine]
    return assemble(mine + theirs, splits, place)


def split_feedforward(pairs, place):
    y, x, c = place
    first = y == 0
    (left_up, right_up), (left_down, right_down) = pairs
    lefts = (jnp.where(first, left_up, left_down), jnp.where(first, left_down, left_up))
    rights = (jnp.where(first, right_up, right_down), jnp.where(first, right_down, right_up))

    def half(c_flip):
        outs = []
        for left, right in zip(lefts, rights):
            blocks = [
                lax.dynamic_slice_in_dim(
                    left, ((x ^ x_flip) * 2 + (c ^ c_flip)) * D, D, axis=1
                )
                for x_flip in range(2)
            ]
            outs.append(rounded(outer_sum(jnp.concatenate(blocks, axis=1), right)))
        return jnp.stack(outs).reshape(2, 2, 2, D // 2, D)

    give = half(1)
    keep = half(0)
    return keep, give


def split_attention(pairs, place):
    y, x, c = place
    lefts = jnp.stack([left for left, _ in pairs])
    mine = y * 2 + x
    inputs_bf, context = pairs[0][1], pairs[3][1]
    rights = jnp.stack([jnp.where((mine ^ flip) == 3, context, inputs_bf) for flip in range(4)])

    def half(c_flip):
        chosen = jnp.concatenate(
            [
                lax.dynamic_slice(
                    lefts, (mine ^ flip, 0, (c ^ c_flip) * (D // 2)), (1, lefts.shape[1], D // 2)
                )
                for flip in range(4)
            ]
        )
        out = lax.dot_general(
            chosen, rights, (((1,), (1,)), ((0,), (0,))), preferred_element_type=jnp.float32
        )
        return rounded(out).reshape(2, 2, 2, D // 4, D)

    give = half(1)
    keep = half(0)
    return keep, give


def spread(values, owners):
    many = values.shape[2]
    lane = jnp.arange(owners * many)
    select = (lane[None, :] % many == jnp.arange(many)[:, None]).astype(jnp.bfloat16)
    wider = jnp.einsum("orf,fn->orn", values, select, preferred_element_type=jnp.float32)
    mine = lane[None, :] // many == jnp.arange(owners)[:, None]
    return jnp.sum(jnp.where(mine[:, None, :], wider, 0.0), axis=0)


def adam_update(master, first, second, grad, rate, decay):
    first_new = BETA_ONE * first + (1.0 - BETA_ONE) * grad
    second_new = BETA_TWO * second + (1.0 - BETA_TWO) * grad * grad
    corr_one = 1.0 - BETA_ONE**ADAM_STEP
    corr_two = 1.0 - BETA_TWO**ADAM_STEP
    update = first_new / corr_one / (jnp.sqrt(second_new / corr_two) + EPS_ADAM)
    return (master - rate * (update + decay * master), first_new, second_new)


def body(
    tokens_in,
    cotangent,
    attention_master,
    feedforward_master,
    vector_master,
    attention_first,
    attention_second,
    feedforward_first,
    feedforward_second,
    vector_first,
    vector_second,
):
    attention_own = attention_master.astype(jnp.bfloat16)
    feedforward_own = feedforward_master.astype(jnp.bfloat16)
    vector_own = vector_master.astype(jnp.bfloat16)
    axes = ("rep", "shard")
    rows = attention_master.shape[0]
    features = vector_master.shape[0] // 12
    own_vector = vector_own.reshape(features, 12)
    vector_rows = jnp.concatenate(
        [
            jnp.pad(jnp.transpose(own_vector[:, :8]), ((0, 0), (0, D - features))),
            jnp.pad(own_vector[:, 8:].reshape(1, 4 * features), ((0, 7), (0, D - 4 * features))),
        ]
    )
    packed = jnp.concatenate([attention_own, vector_rows])
    rep, shard = lax.axis_size("rep"), lax.axis_size("shard")
    tree = rep == 8 and shard == 4
    place = None
    if tree:
        spot = lax.axis_index("rep")
        place = (spot // 4, (spot // 2) % 2, spot % 2)
        column = [packed] + [turn(packed, k) for k in range(1, 4)]
        column, feedforward_own = lax.optimization_barrier((column, feedforward_own))
        wide_column = [feedforward_own] + [turn(feedforward_own, k) for k in range(1, 4)]
        mine = tree_sides(column)
        mine, wide_column = lax.optimization_barrier((mine, wide_column))
        wide_mine = tree_sides(wide_column)
        *attention, vector = tree_gather(mine, ((rows, 4), (16, 1)), place)
        feedforward = tree_gather(wide_mine, ((feedforward_own.shape[0], 2),), place)
        attention = [part.reshape(D, D) for part in attention]
        feedforward = [part.reshape(FF, D) for part in feedforward]
        vector = vector.reshape(32, 16, D)
    else:
        packed = lax.all_gather(packed, axes, axis=0)
        feedforward = lax.all_gather(feedforward_own, axes, axis=0, tiled=True)
        attention = jnp.split(packed[:, :rows].reshape(4 * D, D), 4)
        feedforward = jnp.split(feedforward, 2)
        vector = packed[:, rows:]
    vec = spread(vector[:, :8, :features], rep * shard)
    bias_up = spread(vector[:, 8:9, : 4 * features], rep * shard)[0]
    output, grad_tokens, attention_grad, feedforward_grad, vector_sum = clip_pass(
        tokens_in[0], cotangent[0], attention, feedforward, vec, bias_up, place
    )
    block_out = output[None]
    input_grad = grad_tokens[None]
    owner = lax.axis_index("rep") * shard + lax.axis_index("shard")
    own_rows = lax.dynamic_slice_in_dim(vector_sum[:8], owner * features, features, axis=1)
    own_up = lax.dynamic_slice_in_dim(
        vector_sum[8:].reshape(FF), owner * 4 * features, 4 * features
    )
    vector_grad = jnp.concatenate(
        [jnp.transpose(own_rows), own_up.reshape(features, 4)], axis=1
    ).reshape(-1)
    attention_new, attention_first_new, attention_second_new = adam_update(
        attention_master,
        attention_first,
        attention_second,
        attention_grad,
        RATE_MATRIX,
        DECAY_MATRIX,
    )
    feedforward_new, feedforward_first_new, feedforward_second_new = adam_update(
        feedforward_master,
        feedforward_first,
        feedforward_second,
        feedforward_grad,
        RATE_MATRIX,
        DECAY_MATRIX,
    )
    vector_new, vector_first_new, vector_second_new = adam_update(
        vector_master, vector_first, vector_second, vector_grad, RATE_VECTOR, 0.0
    )
    return (
        block_out,
        input_grad,
        attention_grad,
        feedforward_grad,
        vector_grad,
        attention_new,
        feedforward_new,
        vector_new,
        attention_first_new,
        attention_second_new,
        feedforward_first_new,
        feedforward_second_new,
        vector_first_new,
        vector_second_new,
    )


def solution(mesh):
    placed = (
        P(("rep", "shard"), None, None),
        P(("rep", "shard"), None, None),
        P(("rep", "shard"), None),
        P(("rep", "shard"), None),
        P(("rep", "shard")),
        P(("rep", "shard"), None),
        P(("rep", "shard"), None),
        P(("rep", "shard"), None),
        P(("rep", "shard"), None),
        P(("rep", "shard")),
        P(("rep", "shard")),
    )
    return jax.shard_map(
        body,
        mesh=mesh,
        in_specs=placed,
        out_specs=(
            P(("rep", "shard"), None, None),
            P(("rep", "shard"), None, None),
            P(("rep", "shard"), None),
            P(("rep", "shard"), None),
            P(("rep", "shard")),
            P(("rep", "shard"), None),
            P(("rep", "shard"), None),
            P(("rep", "shard")),
            P(("rep", "shard"), None),
            P(("rep", "shard"), None),
            P(("rep", "shard"), None),
            P(("rep", "shard"), None),
            P(("rep", "shard")),
            P(("rep", "shard")),
        ),
        check_vma=False,
    )
```

```python
import jax
import jax.numpy as jnp
from jax import lax
from jax.experimental import pallas as pl
from jax.experimental.pallas import tpu as pltpu
from jax.sharding import PartitionSpec as P

D = 768
HEADS = 12
HD = 64
FF = 3072
ADAM_STEP = 2


EPS_NORM = 1e-05
EPS_ADAM = 1e-08
BETA_ONE = 0.9
BETA_TWO = 0.95
RATE_MATRIX = 0.01
RATE_VECTOR = 0.05
DECAY_MATRIX = 0.01


def mix(form, left, right):
    return jnp.einsum(form, left, right, preferred_element_type=jnp.float32)


def times_trans(left, right):
    return lax.dot_general(
        left, right, (((1,), (1,)), ((), ())), preferred_element_type=jnp.float32
    )


def outer_sum(left, right):
    return lax.dot_general(
        left, right, (((0,), (0,)), ((), ())), preferred_element_type=jnp.float32
    )


def layer_norm(field, gain, shift):
    center = field - jnp.mean(field, axis=-1, keepdims=True)
    inverse = lax.rsqrt(jnp.mean(center * center, axis=-1, keepdims=True) + EPS_NORM)
    normed = center * inverse
    return (normed * gain + shift, normed, inverse)


def norm_back(upstream, normed, inverse, gain):
    scaled = upstream * gain
    return inverse * (
        scaled
        - jnp.mean(scaled, axis=-1, keepdims=True)
        - normed * jnp.mean(scaled * normed, axis=-1, keepdims=True)
    )


def gelu_value(pre):
    return 0.5 * pre * (1.0 + lax.erf(pre * 0.7071067811865476))


def gelu_slope(pre):
    return (
        0.5 * (1.0 + lax.erf(pre * 0.7071067811865476))
        + pre * jnp.exp(-0.5 * pre * pre) * 0.3989422804014327
    )


def clip_pass(tokens, upstream, attention, feedforward, vec, bias_up, place):
    frames = tokens.shape[0]
    scale = HD ** (-0.5)
    gain_one, shift_one, bias_query, bias_value = vec[0], vec[1], vec[2], vec[3]
    bias_out, gain_two, shift_two, bias_down = vec[4], vec[5], vec[6], vec[7]
    w_query, w_key, w_value, w_out = attention
    tree = place is not None
    normed_out, normed_one, inverse_one = layer_norm(tokens, gain_one, shift_one)
    inputs_bf = normed_out.astype(jnp.bfloat16)
    queries = (
        (times_trans(inputs_bf, w_query) + bias_query)
        .astype(jnp.bfloat16)
        .reshape(frames, HEADS, HD)
    )
    keys_bf = times_trans(inputs_bf, w_key).astype(jnp.bfloat16).reshape(frames, HEADS, HD)
    values_bf = (
        (times_trans(inputs_bf, w_value) + bias_value)
        .astype(jnp.bfloat16)
        .reshape(frames, HEADS, HD)
    )
    if tree:
        feedforward, (queries, keys_bf, values_bf) = feedforward((queries, keys_bf, values_bf))
    w_up, w_down = feedforward
    scores = mix("qhd,khd->hqk", queries, keys_bf) * scale
    top = jnp.max(scores, axis=-1, keepdims=True)
    lse = top + jnp.log(jnp.sum(jnp.exp(scores - top), axis=-1, keepdims=True))
    weights_bf = jnp.exp(scores - lse).astype(jnp.bfloat16)
    context = mix("hqk,khd->qhd", weights_bf, values_bf).reshape(frames, D).astype(jnp.bfloat16)
    resid = tokens + times_trans(context, w_out) + bias_out
    normed_out_two, normed_two, inverse_two = layer_norm(resid, gain_two, shift_two)
    mlp_in = normed_out_two.astype(jnp.bfloat16)
    pre = times_trans(mlp_in, w_up) + bias_up
    active = gelu_value(pre).astype(jnp.bfloat16)
    output = resid + jnp.dot(active, w_down, preferred_element_type=jnp.float32) + bias_down
    upstream_bf = upstream.astype(jnp.bfloat16)
    grad_bias_down = jnp.sum(upstream, axis=0)
    grad_pre = times_trans(upstream_bf, w_down) * gelu_slope(pre)
    grad_pre_bf = grad_pre.astype(jnp.bfloat16)
    grad_bias_up = jnp.sum(grad_pre, axis=0)
    feedforward_pairs = [(grad_pre_bf, mlp_in), (active, upstream_bf)]
    feedforward_grad = attention_grad = None
    if tree:
        keep, give = split_feedforward(feedforward_pairs, place)
        keep, give, grad_pre_bf = lax.optimization_barrier((keep, give, grad_pre_bf))
        got = hop(give, 1)
    grad_normed_two = jnp.dot(grad_pre_bf, w_up, preferred_element_type=jnp.float32)
    grad_gain_two = jnp.sum(grad_normed_two * normed_two, axis=0)
    grad_shift_two = jnp.sum(grad_normed_two, axis=0)
    grad_resid = upstream + norm_back(grad_normed_two, normed_two, inverse_two, gain_two)
    resid_bf = grad_resid.astype(jnp.bfloat16)
    grad_context = jnp.dot(resid_bf, w_out, preferred_element_type=jnp.float32).astype(jnp.bfloat16)
    if tree:
        got, resid_bf, grad_context = lax.optimization_barrier((got, resid_bf, grad_context))
        total = rounded(wide(keep) + wide(got))
        total, grad_context = lax.optimization_barrier((total, grad_context))
        got_a, got_b = tree_middle(total)
    again = mix("qhd,khd->hqk", queries, keys_bf) * scale
    probs = jnp.exp(again - lse)
    probs_bf = probs.astype(jnp.bfloat16)
    context_heads = grad_context.reshape(frames, HEADS, HD)
    delta = jnp.sum(
        grad_context.astype(jnp.float32).reshape(frames, HEADS, HD)
        * context.astype(jnp.float32).reshape(frames, HEADS, HD),
        axis=-1,
    )
    delta = jnp.transpose(delta)[:, :, None]
    grad_values = mix("hqk,qhd->khd", probs_bf, context_heads).reshape(frames, D)
    grad_probs = mix("qhd,khd->hqk", context_heads, values_bf)
    grad_scores = (probs * (grad_probs - delta)).astype(jnp.bfloat16)
    grad_queries = (mix("hqk,khd->qhd", grad_scores, keys_bf) * scale).reshape(frames, D)
    grad_keys = (mix("hqk,qhd->khd", grad_scores, queries) * scale).reshape(frames, D)
    queries_grad_bf = grad_queries.astype(jnp.bfloat16)
    keys_grad_bf = grad_keys.astype(jnp.bfloat16)
    values_grad_bf = grad_values.astype(jnp.bfloat16)
    attention_pairs = [
        (queries_grad_bf, inputs_bf),
        (keys_grad_bf, inputs_bf),
        (values_grad_bf, inputs_bf),
        (resid_bf, context),
    ]
    if tree:
        keep, give = split_attention(attention_pairs, place)
        keep, give, got_a, got_b, output = lax.optimization_barrier(
            (keep, give, got_a, got_b, output)
        )
        got = hop(give, 1)
        sums = tree_sums(total, got_a, got_b)
        lasts = tree_last(sums)
        sums, queries_grad_bf, got = lax.optimization_barrier((sums, queries_grad_bf, got))
        total = rounded(wide(keep) + wide(got))
        got_a, got_b = tree_middle(total)
        (
            total,
            queries_grad_bf,
            grad_queries,
            grad_values,
            grad_gain_two,
            grad_shift_two,
            grad_resid,
            grad_bias_down,
            grad_bias_up,
        ) = lax.optimization_barrier(
            (
                total,
                queries_grad_bf,
                grad_queries,
                grad_values,
                grad_gain_two,
                grad_shift_two,
                grad_resid,
                grad_bias_down,
                grad_bias_up,
            )
        )
    grad_bias_query = jnp.sum(grad_queries, axis=0)
    grad_bias_value = jnp.sum(grad_values, axis=0)
    grad_bias_out = jnp.sum(grad_resid, axis=0)
    grad_normed_one = (
        jnp.dot(queries_grad_bf, w_query, preferred_element_type=jnp.float32)
        + jnp.dot(keys_grad_bf, w_key, preferred_element_type=jnp.float32)
        + jnp.dot(values_grad_bf, w_value, preferred_element_type=jnp.float32)
    )
    grad_gain_one = jnp.sum(grad_normed_one * normed_one, axis=0)
    grad_shift_one = jnp.sum(grad_normed_one, axis=0)
    grad_tokens = grad_resid + norm_back(grad_normed_one, normed_one, inverse_one, gain_one)
    rows = jnp.stack(
        [
            grad_gain_one,
            grad_shift_one,
            grad_bias_query,
            grad_bias_value,
            grad_bias_out,
            grad_gain_two,
            grad_shift_two,
            grad_bias_down,
        ],
        axis=0,
    )
    vector_part = jnp.concatenate([rows, grad_bias_up.reshape(FF // D, D)], axis=0)
    if tree:
        got_a, got_b, lasts, vector_part, grad_tokens = lax.optimization_barrier(
            (got_a, got_b, lasts, vector_part, grad_tokens)
        )
        blocks = tree_blocks(tree_own(sums, lasts))
        blocks, got_a, got_b, vector_part = lax.optimization_barrier(
            (blocks, got_a, got_b, vector_part)
        )
        feedforward_parts = tree_column(blocks)
        sums = tree_sums(total, got_a, got_b)
        lasts = tree_last(sums)
        vector_part = vector_part + sum(hop(vector_part, flip) for flip in range(1, 8))
        lasts, feedforward_parts, vector_part = lax.optimization_barrier(
            (lasts, feedforward_parts, vector_part)
        )
        attention_parts = tree_column(tree_blocks(tree_own(sums, lasts)))
        vector_sum = vector_part + sum(turn(vector_part, step) for step in range(1, 4))
        feedforward_grad = sum(wide(part) for part in feedforward_parts)
        attention_grad = sum(wide(part) for part in attention_parts)
    else:
        feedforward_grad, attention_grad = [
            wide(
                lax.psum_scatter(
                    rounded(jnp.concatenate([outer_sum(*pair) for pair in pairs])),
                    ("rep", "shard"),
                    scatter_dimension=0,
                    tiled=True,
                )
            )
            for pairs in (feedforward_pairs, attention_pairs)
        ]
        vector_sum = lax.psum(vector_part, ("rep", "shard"))
    return (output, grad_tokens, attention_grad, feedforward_grad, vector_sum)


def hop(value, bit):
    return lax.ppermute(value, "rep", [(r, r ^ bit) for r in range(8)])


def rounded(value):
    return value.astype(jnp.bfloat16)


def wide(value):
    return value.astype(jnp.float32)


def tree_middle(total):
    return hop(total[:, 1, 0], 2), hop(total[1, :, 1], 4)


def tree_sums(total, got_a, got_b):
    sum_a = rounded(wide(total[:, 0, 0]) + wide(got_a))
    sum_b = rounded(wide(total[0, :, 1]) + wide(got_b))
    return sum_a, sum_b


def tree_last(sums):
    return hop(sums[0][1], 4), hop(sums[1][1], 2)


def tree_own(sums, lasts):
    own = jnp.stack([wide(part[0]) + wide(last) for part, last in zip(sums, lasts)])
    return rounded(own).reshape(4, -1, D)


def turn(value, step):
    return lax.ppermute(value, "shard", [(z, (z + step) % 4) for z in range(4)])


def tree_blocks(own):
    z = lax.axis_index("shard")
    return [lax.dynamic_index_in_dim(own, (z + 4 - k) % 4, 0, False) for k in range(4)]


def tree_column(blocks):
    return [blocks[0]] + [turn(blocks[k], -k) for k in range(1, 4)]


FLIPS = ((0, 0, 0, 4), (0, 1, 0, 4), (1, 0, 0, 4), (1, 1, 0, 2), (1, 1, 2, 4))


def assemble(pieces, splits, place):
    y, x, c = place
    count = len(pieces) * len(splits)
    spots = jnp.stack(
        [
            ((y ^ y_flip) * 2 + (x ^ x_flip)) * 2 + (c ^ c_flip)
            for c_flip in range(2)
            for y_flip, x_flip, _, _ in FLIPS
        ]
    ).astype(jnp.int32)

    def kernel(spots_ref, *refs):
        ins, outs, sems = refs[: len(pieces)], refs[len(pieces) : -1], refs[-1]

        def copy_of(at, part, group):
            _, _, low, high = FLIPS[at % len(FLIPS)]
            rows, groups = splits[part]
            first = sum(many for _, many in splits[:part])
            return pltpu.make_async_copy(
                ins[at].at[:, pl.ds(sum(many for many, _ in splits[:part]), rows)],
                outs[first + group].at[spots_ref[at] % (8 // groups), pl.ds(low, high - low)],
                sems.at[at * len(splits) + part],
            )

        jobs = [(at, part) for at in range(len(pieces)) for part in range(len(splits))]
        for at, part in jobs:
            groups = splits[part][1]
            for group in range(groups):

                @pl.when(spots_ref[at] // (8 // groups) == group)
                def _():
                    copy_of(at, part, group).start()

        for at, part in jobs:
            copy_of(at, part, 0).wait()

    return pl.pallas_call(
        kernel,
        out_shape=[
            jax.ShapeDtypeStruct((8 // groups, 4, rows, D), jnp.bfloat16)
            for rows, groups in splits
            for _ in range(groups)
        ],
        in_specs=[pl.BlockSpec(memory_space=pltpu.SMEM)]
        + [pl.BlockSpec(memory_space=pl.ANY)] * len(pieces),
        out_specs=[pl.BlockSpec(memory_space=pltpu.VMEM)] * sum(groups for _, groups in splits),
        scratch_shapes=[pltpu.SemaphoreType.DMA((count,))],
        compiler_params=pltpu.CompilerParams(vmem_limit_bytes=24 * 1024 * 1024),
    )(spots, *pieces)


def stack_column(blocks):
    z = lax.axis_index("shard")
    spots = jnp.stack([(z + 4 - k) % 4 for k in range(4)]).astype(jnp.int32)

    def kernel(spots_ref, *refs):
        ins, out, sems = refs[:4], refs[4], refs[5]
        copies = [
            pltpu.make_async_copy(ins[k], out.at[spots_ref[k]], sems.at[k]) for k in range(4)
        ]
        for copy in copies:
            copy.start()
        for copy in copies:
            copy.wait()

    return pl.pallas_call(
        kernel,
        out_shape=jax.ShapeDtypeStruct((4,) + blocks[0].shape, jnp.bfloat16),
        in_specs=[pl.BlockSpec(memory_space=pltpu.SMEM)]
        + [pl.BlockSpec(memory_space=pl.ANY)] * 4,
        out_specs=pl.BlockSpec(memory_space=pltpu.VMEM),
        scratch_shapes=[pltpu.SemaphoreType.DMA((4,))],
        compiler_params=pltpu.CompilerParams(vmem_limit_bytes=8 * 1024 * 1024),
    )(spots, *blocks)


def tree_sides(column):
    return [column, hop(column, 2), hop(column, 4)]


def tree_gather(mine, splits, place):
    _, by_x, by_y = mine
    mine = mine + [hop(by_y[:2], 2), hop(by_x[2:], 4)]
    theirs = [hop(part, 1) for part in mine]
    return assemble(mine + theirs, splits, place)


def split_feedforward(pairs, place):
    y, x, c = place
    first = y == 0
    (left_up, right_up), (left_down, right_down) = pairs
    lefts = (jnp.where(first, left_up, left_down), jnp.where(first, left_down, left_up))
    rights = (jnp.where(first, right_up, right_down), jnp.where(first, right_down, right_up))

    def half(c_flip):
        outs = []
        for left, right in zip(lefts, rights):
            blocks = [
                lax.dynamic_slice_in_dim(
                    left, ((x ^ x_flip) * 2 + (c ^ c_flip)) * D, D, axis=1
                )
                for x_flip in range(2)
            ]
            outs.append(rounded(outer_sum(jnp.concatenate(blocks, axis=1), right)))
        return jnp.stack(outs).reshape(2, 2, 2, D // 2, D)

    give = half(1)
    keep = half(0)
    return keep, give


def split_attention(pairs, place):
    y, x, c = place
    lefts = jnp.stack([left for left, _ in pairs])
    mine = y * 2 + x
    inputs_bf, context = pairs[0][1], pairs[3][1]
    rights = jnp.stack([jnp.where((mine ^ flip) == 3, context, inputs_bf) for flip in range(4)])

    def half(c_flip):
        chosen = jnp.concatenate(
            [
                lax.dynamic_slice(
                    lefts, (mine ^ flip, 0, (c ^ c_flip) * (D // 2)), (1, lefts.shape[1], D // 2)
                )
                for flip in range(4)
            ]
        )
        out = lax.dot_general(
            chosen, rights, (((1,), (1,)), ((0,), (0,))), preferred_element_type=jnp.float32
        )
        return rounded(out).reshape(2, 2, 2, D // 4, D)

    give = half(1)
    keep = half(0)
    return keep, give


def spread(values, owners):
    many = values.shape[2]
    lane = jnp.arange(owners * many)
    select = (lane[None, :] % many == jnp.arange(many)[:, None]).astype(jnp.bfloat16)
    wider = jnp.einsum("orf,fn->orn", values, select, preferred_element_type=jnp.float32)
    mine = lane[None, :] // many == jnp.arange(owners)[:, None]
    return jnp.sum(jnp.where(mine[:, None, :], wider, 0.0), axis=0)


def adam_update(master, first, second, grad, rate, decay):
    first_new = BETA_ONE * first + (1.0 - BETA_ONE) * grad
    second_new = BETA_TWO * second + (1.0 - BETA_TWO) * grad * grad
    corr_one = 1.0 - BETA_ONE**ADAM_STEP
    corr_two = 1.0 - BETA_TWO**ADAM_STEP
    update = first_new / corr_one / (jnp.sqrt(second_new / corr_two) + EPS_ADAM)
    return (master - rate * (update + decay * master), first_new, second_new)


def body(
    tokens_in,
    cotangent,
    attention_master,
    feedforward_master,
    vector_master,
    attention_first,
    attention_second,
    feedforward_first,
    feedforward_second,
    vector_first,
    vector_second,
):
    attention_own = attention_master.astype(jnp.bfloat16)
    feedforward_own = feedforward_master.astype(jnp.bfloat16)
    vector_own = vector_master.astype(jnp.bfloat16)
    axes = ("rep", "shard")
    rows = attention_master.shape[0]
    features = vector_master.shape[0] // 12
    own_vector = vector_own.reshape(features, 12)
    vector_rows = jnp.concatenate(
        [
            jnp.pad(jnp.transpose(own_vector[:, :8]), ((0, 0), (0, D - features))),
            jnp.pad(own_vector[:, 8:].reshape(1, 4 * features), ((0, 7), (0, D - 4 * features))),
        ]
    )
    packed = jnp.concatenate([attention_own, vector_rows])
    rep, shard = lax.axis_size("rep"), lax.axis_size("shard")
    tree = rep == 8 and shard == 4
    place = None
    if tree:
        spot = lax.axis_index("rep")
        place = (spot // 4, (spot // 2) % 2, spot % 2)
        column = [packed] + [turn(packed, k) for k in range(1, 4)]
        column, feedforward_own = lax.optimization_barrier((column, feedforward_own))
        wide_column = [feedforward_own] + [turn(feedforward_own, k) for k in range(1, 4)]
        mine = tree_sides(stack_column(column))
        mine, wide_column = lax.optimization_barrier((mine, wide_column))
        wide_mine = tree_sides(stack_column(wide_column))
        *attention, vector = tree_gather(mine, ((rows, 4), (16, 1)), place)

        def late(values):
            sides, values = lax.optimization_barrier((wide_mine, values))
            spread_rows = ((feedforward_own.shape[0], 2),)
            parts = tree_gather(sides, spread_rows, place)
            return [part.reshape(FF, D) for part in parts], values

        feedforward = late
        attention = [part.reshape(D, D) for part in attention]
        vector = vector.reshape(32, 16, D)
    else:
        packed = lax.all_gather(packed, axes, axis=0)
        feedforward = lax.all_gather(feedforward_own, axes, axis=0, tiled=True)
        attention = jnp.split(packed[:, :rows].reshape(4 * D, D), 4)
        feedforward = jnp.split(feedforward, 2)
        vector = packed[:, rows:]
    vec = spread(vector[:, :8, :features], rep * shard)
    bias_up = spread(vector[:, 8:9, : 4 * features], rep * shard)[0]
    output, grad_tokens, attention_grad, feedforward_grad, vector_sum = clip_pass(
        tokens_in[0], cotangent[0], attention, feedforward, vec, bias_up, place
    )
    block_out = output[None]
    input_grad = grad_tokens[None]
    owner = lax.axis_index("rep") * shard + lax.axis_index("shard")
    own_rows = lax.dynamic_slice_in_dim(vector_sum[:8], owner * features, features, axis=1)
    own_up = lax.dynamic_slice_in_dim(
        vector_sum[8:].reshape(FF), owner * 4 * features, 4 * features
    )
    vector_grad = jnp.concatenate(
        [jnp.transpose(own_rows), own_up.reshape(features, 4)], axis=1
    ).reshape(-1)
    attention_new, attention_first_new, attention_second_new = adam_update(
        attention_master,
        attention_first,
        attention_second,
        attention_grad,
        RATE_MATRIX,
        DECAY_MATRIX,
    )
    feedforward_new, feedforward_first_new, feedforward_second_new = adam_update(
        feedforward_master,
        feedforward_first,
        feedforward_second,
        feedforward_grad,
        RATE_MATRIX,
        DECAY_MATRIX,
    )
    vector_new, vector_first_new, vector_second_new = adam_update(
        vector_master, vector_first, vector_second, vector_grad, RATE_VECTOR, 0.0
    )
    return (
        block_out,
        input_grad,
        attention_grad,
        feedforward_grad,
        vector_grad,
        attention_new,
        feedforward_new,
        vector_new,
        attention_first_new,
        attention_second_new,
        feedforward_first_new,
        feedforward_second_new,
        vector_first_new,
        vector_second_new,
    )


def solution(mesh):
    placed = (
        P(("rep", "shard"), None, None),
        P(("rep", "shard"), None, None),
        P(("rep", "shard"), None),
        P(("rep", "shard"), None),
        P(("rep", "shard")),
        P(("rep", "shard"), None),
        P(("rep", "shard"), None),
        P(("rep", "shard"), None),
        P(("rep", "shard"), None),
        P(("rep", "shard")),
        P(("rep", "shard")),
    )
    return jax.shard_map(
        body,
        mesh=mesh,
        in_specs=placed,
        out_specs=(
            P(("rep", "shard"), None, None),
            P(("rep", "shard"), None, None),
            P(("rep", "shard"), None),
            P(("rep", "shard"), None),
            P(("rep", "shard")),
            P(("rep", "shard"), None),
            P(("rep", "shard"), None),
            P(("rep", "shard")),
            P(("rep", "shard"), None),
            P(("rep", "shard"), None),
            P(("rep", "shard"), None),
            P(("rep", "shard"), None),
            P(("rep", "shard")),
            P(("rep", "shard")),
        ),
        check_vma=False,
    )
```
